32 devices in a mesh: dp: 2 (over x), row: 4 (over z), col: 4 (over y, core).
Axes of the slice: x: 2, y: 2, z: 4, core: 2. Of those that a mesh axis runs over, the one named last changes fastest.
Arguments:
- block_input: float32 [1024, 768], P(('dp', 'col'), 'row'), may hold values from -6 to 6
- seq_lens: int32 [2, 4], P('dp'), may hold values from 0 to 512, as said below
- seq_offsets: int32 [2, 4], P('dp'), may hold values from 0 to 4, as said below
- ln_gain: float32 [2, 2, 768], P(None, None, 'row'), may hold values from 0.5 to 1.5
- ln_bias: float32 [2, 2, 768], P(None, None, 'row'), may hold values from -1.2 to 1.2
- w_qkv: bfloat16 [2, 768, 2304], P(None, 'row', 'col'), may hold values from -0.5 to 0.5
- w_attn_out: bfloat16 [2, 768, 768], P(None, 'col', 'row'), may hold values from -0.875 to 0.875
- w_up: bfloat16 [2, 768, 3072], P(None, 'row', 'col'), may hold values from -0.21875 to 0.21875
- w_down: bfloat16 [2, 3072, 768], P(None, 'col', 'row'), may hold values from -0.109375 to 0.109375
- cotangent: float32 [1024, 768], P(('dp', 'col'), 'row'), may hold values from -6 to 6
Outputs:
- block_output: float32 [1024, 768], P(('dp', 'col'), 'row')
- grad_input: float32 [1024, 768], P(('dp', 'col'), 'row')
- grad_ln_gain: float32 [2, 2, 768], P(None, None, 'row')
- grad_ln_bias: float32 [2, 2, 768], P(None, None, 'row')
- grad_w_qkv: float32 [2, 768, 2304], P(None, 'row', 'col')
- grad_w_attn_out: float32 [2, 768, 768], P(None, 'col', 'row')
- grad_w_up: float32 [2, 768, 3072], P(None, 'row', 'col')
- grad_w_down: float32 [2, 3072, 768], P(None, 'col', 'row')
The draws below stay inside these ranges and needn't reach their ends.
Inputs may be any that keep to these rules, and one draw needn't show every extreme that they name: Slot s of data shard r holds a sequence of seq_lens[r, s] tokens that starts at padding block seq_offsets[r, s]. Used slots come first with rising offsets from 0; each sequence owns the blocks up to the next used slot's offset (the last one up to 4), and its last block holds 1 to 128 of its tokens. Unused slots have length 0. `seq_offsets`: unused slots have offset 4.
All inputs are finite; a program needn't handle non-finite values.
Results may differ from the reference program's by a relative error of at most 0.03.
Values may be sent and summed in bfloat16 or wider, within the bound.
A program may use at most 64 MiB of HBM per device.

```python
import math
import jax
import jax.numpy as jnp
from jax import lax

D = 768
HD = 64
FF = 3072
ROT = 16
LAYERS = 2
BLOCK = 128
TOK_DP = 512
BLOCKS = 4
TOKENS = 1024
N_DP = 2


def layout_draw(key):
    cut_key = jax.random.fold_in(key, 11)
    tail_key = jax.random.fold_in(key, 12)
    shard_ids = jnp.arange(N_DP, dtype=jnp.int32)[:, None]
    cut_flags = jax.random.randint(cut_key, (N_DP, BLOCKS - 1), 0, 2).astype(jnp.int32)
    cut_flags = jnp.where(shard_ids == 0, 0, cut_flags)
    start_flags = jnp.concatenate([jnp.ones((N_DP, 1), jnp.int32), cut_flags], axis=1)
    owner_slot = jnp.cumsum(start_flags, axis=1) - 1
    slot_ids = jnp.arange(BLOCKS, dtype=jnp.int32)
    member = owner_slot[:, None, :] == slot_ids[None, :, None]
    counts = jnp.sum(member.astype(jnp.int32), axis=2)
    offsets = jnp.min(jnp.where(member, slot_ids[None, None, :], BLOCKS), axis=2)
    tail_tokens = jax.random.randint(tail_key, (N_DP, BLOCKS), 1, BLOCK + 1).astype(jnp.int32)
    tail_tokens = jnp.where((shard_ids == 0) & (slot_ids[None, :] == 0), BLOCK, tail_tokens)
    lengths = jnp.where(counts > 0, BLOCK * (counts - 1) + tail_tokens, 0)
    return (lengths.astype(jnp.int32), offsets.astype(jnp.int32))


def draw_seq_lens(key, part):
    return layout_draw(key)[0]


def draw_seq_offsets(key, part):
    return layout_draw(key)[1]


def draw_w_qkv(key, part):
    base_key = jax.random.fold_in(key, 31)
    spread = float(D) ** (-0.5)
    weights = jax.random.normal(base_key, (LAYERS, D, 3 * D), jnp.float32) * spread
    return jnp.clip(weights, -0.5, 0.5).astype(jnp.bfloat16)


def level_of(rng, shape, cuts, low, largest):
    def one(dim, shards_of):
        heights = jax.random.uniform(jax.random.fold_in(jax.random.fold_in(rng, 6), dim), (shards_of,), jnp.float32, low / len(cuts), largest / len(cuts))
        return jnp.repeat(jnp.exp(heights), shape[dim] // shards_of).reshape((-1,) + (1,) * (len(shape) - dim - 1))

    loudness = one(*cuts[0])
    for cut in cuts[1:]:
        loudness = loudness * one(*cut)
    return loudness


def gaussian(own_key, extent, deviation, reach, pieces=(), held_as=jnp.bfloat16):
    factor_of = level_of(own_key, extent, pieces, -0.22, 0.18) if pieces else 1.0
    drawn = jax.random.normal(own_key, extent, jnp.float32) * deviation * factor_of
    return jnp.minimum(jnp.maximum(drawn, -reach), reach).astype(held_as)


def setup_inputs(seed: int = 0) -> dict:
    arg_keys = jax.random.split(jax.random.key(seed), 11)
    return {
        "block_input": gaussian(arg_keys[0], (TOKENS, D), 1.0, 6.0, ((0, 8), (1, 4)), jnp.float32),
        "seq_lens": draw_seq_lens(jax.random.fold_in(arg_keys[10], 71), 0),
        "seq_offsets": draw_seq_offsets(jax.random.fold_in(arg_keys[10], 71), 0),
        "ln_gain": jnp.clip(1.0 + 0.1 * jax.random.normal(arg_keys[3], (LAYERS, 2, D), jnp.float32), 0.5, 1.5),
        "ln_bias": gaussian(arg_keys[4], (LAYERS, 2, D), 0.2, 1.2, ((2, 4),), jnp.float32),
        "w_qkv": draw_w_qkv(jax.random.fold_in(arg_keys[10], 71), 0),
        "w_attn_out": gaussian(arg_keys[6], (LAYERS, D, D), (D // 16) ** -0.5, 0.875, ((1, 4), (2, 4))),
        "w_up": gaussian(arg_keys[7], (LAYERS, D, FF), D ** -0.5, 0.21875, ((1, 4), (2, 4))),
        "w_down": gaussian(arg_keys[8], (LAYERS, FF, D), FF ** -0.5, 0.109375, ((1, 4), (2, 4))),
        "cotangent": gaussian(arg_keys[9], (TOKENS, D), 1.0, 6.0, ((0, 8), (1, 4)), jnp.float32),
    }


EPSILON = 1e-05
NEG_LARGE = -1e+30

def token_layout(lengths, offsets, token_total):
    tokens = jnp.arange(token_total, dtype=jnp.int32)
    block_of = tokens // BLOCK
    slot_ids = jnp.arange(lengths.shape[0], dtype=jnp.int32)
    begun_flags = (offsets[None, :] <= block_of[:, None]).astype(jnp.int32)
    segment = lax.optimization_barrier(jnp.sum(begun_flags, axis=1)) - 1
    picked = (slot_ids[None, :] == segment[:, None]).astype(jnp.int32)
    first_block = lax.optimization_barrier(jnp.sum(picked * offsets[None, :], axis=1))
    seq_length = lax.optimization_barrier(jnp.sum(picked * lengths[None, :], axis=1))
    position = tokens - first_block * BLOCK
    return (segment, position, position < seq_length)

def rotary_tables(position):
    half_rot = ROT // 2
    frequency = jnp.exp(jnp.arange(half_rot, dtype=jnp.float32) * (-2.0 * math.log(10000.0) / ROT))
    angles = position.astype(jnp.float32)[:, None] * frequency[None, :]
    return (jnp.cos(angles), jnp.sin(angles))

def rotate_pairs(head_values, cosine_table, sine_table, direction):
    half_rot = ROT // 2
    lead_half = head_values[..., :half_rot]
    next_half = head_values[..., half_rot:ROT]
    tail_dims = head_values[..., ROT:]
    cos_wide = cosine_table[:, None, :]
    sin_wide = sine_table[:, None, :] * direction
    return jnp.concatenate([lead_half * cos_wide - next_half * sin_wide, next_half * cos_wide + lead_half * sin_wide, tail_dims], axis=-1)

def rotary_pack(projected, cosine_table, sine_table):
    row_total = projected.shape[0]
    head_total = projected.shape[1] // (3 * HD)
    head_grid = projected.reshape(row_total, head_total, 3, HD)
    turned_q = rotate_pairs(head_grid[:, :, 0], cosine_table, sine_table, 1.0)
    turned_k = rotate_pairs(head_grid[:, :, 1], cosine_table, sine_table, 1.0)
    head_grid = jnp.stack([turned_q, turned_k, head_grid[:, :, 2]], axis=2)
    return head_grid.reshape(row_total, -1).astype(jnp.bfloat16)

def split_heads(packed):
    row_total = packed.shape[0]
    head_total = packed.shape[1] // (3 * HD)
    head_grid = packed.reshape(row_total, head_total, 3, HD)
    return (head_grid[:, :, 0], head_grid[:, :, 1], head_grid[:, :, 2])

def gelu_exact(pre_value):
    return 0.5 * pre_value * (1.0 + jax.scipy.special.erf(pre_value / math.sqrt(2.0)))

def gelu_slope(pre_value):
    cumulative = 0.5 * (1.0 + jax.scipy.special.erf(pre_value / math.sqrt(2.0)))
    return cumulative + pre_value * jnp.exp(-0.5 * pre_value * pre_value) / math.sqrt(2.0 * math.pi)

def score_rows(token_total):
    return token_total if token_total <= 1024 else 512

def allowed_block(row_start, row_count, segment, is_valid):
    row_ids = row_start + jnp.arange(row_count, dtype=jnp.int32)
    columns = jnp.arange(segment.shape[0], dtype=jnp.int32)
    seg_rows = lax.dynamic_slice_in_dim(segment, row_start, row_count)
    inside = (seg_rows[:, None] == segment[None, :]) & (columns[None, :] <= row_ids[:, None]) & is_valid[None, :]
    return inside | (columns[None, :] == row_ids[:, None])

def attend_forward(queries, key_rows, values, segment, is_valid):
    token_total = queries.shape[0]
    head_total = queries.shape[1]
    block_rows = score_rows(token_total)
    score_scale = 1.0 / math.sqrt(HD)
    keys_wide = key_rows.astype(jnp.float32)
    values_wide = values.astype(jnp.float32)

    def one_block(block_index):
        row_start = block_index * block_rows
        query_block = lax.dynamic_slice_in_dim(queries, row_start, block_rows, 0).astype(jnp.float32)
        scores = jnp.einsum('qhd,khd->hqk', query_block, keys_wide) * score_scale
        allowed = allowed_block(row_start, block_rows, segment, is_valid)
        scores = jnp.where(allowed[None], scores, NEG_LARGE)
        top_score = lax.optimization_barrier(jnp.max(scores, axis=2, keepdims=True))
        log_total = top_score + jnp.log(lax.optimization_barrier(jnp.sum(jnp.exp(scores - top_score), axis=2, keepdims=True)))
        prob_low = lax.optimization_barrier(jnp.exp(scores - log_total).astype(jnp.bfloat16))
        attended = jnp.einsum('hqk,khd->qhd', prob_low.astype(jnp.float32), values_wide)
        return (attended.astype(jnp.bfloat16), log_total[:, :, 0])
    block_ids = jnp.arange(token_total // block_rows, dtype=jnp.int32)
    attended, log_total = lax.map(one_block, block_ids)
    return (attended.reshape(token_total, head_total, HD), log_total)

def attend_backward(queries, key_rows, values, attended, grad_att, log_total, segment, is_valid):
    token_total = queries.shape[0]
    head_total = queries.shape[1]
    block_rows = score_rows(token_total)
    score_scale = 1.0 / math.sqrt(HD)
    keys_wide = key_rows.astype(jnp.float32)
    values_wide = values.astype(jnp.float32)

    def one_block(running, block_inputs):
        key_grad, value_grad = running
        block_index, block_log = block_inputs
        row_start = block_index * block_rows
        query_block = lax.dynamic_slice_in_dim(queries, row_start, block_rows, 0).astype(jnp.float32)
        grad_block = lax.dynamic_slice_in_dim(grad_att, row_start, block_rows, 0).astype(jnp.float32)
        out_block = lax.dynamic_slice_in_dim(attended, row_start, block_rows, 0).astype(jnp.float32)
        scores = jnp.einsum('qhd,khd->hqk', query_block, keys_wide) * score_scale
        allowed = allowed_block(row_start, block_rows, segment, is_valid)
        scores = jnp.where(allowed[None], scores, NEG_LARGE)
        prob_table = jnp.exp(scores - block_log[:, :, None])
        prob_low = lax.optimization_barrier(prob_table.astype(jnp.bfloat16)).astype(jnp.float32)
        value_grad = value_grad + jnp.einsum('hqk,qhd->khd', prob_low, grad_block)
        weight_grad = jnp.einsum('qhd,khd->hqk', grad_block, values_wide)
        row_delta = jnp.transpose(lax.optimization_barrier(jnp.sum(grad_block * out_block, axis=2)))
        score_grad = (prob_table * (weight_grad - row_delta[:, :, None]) * score_scale).astype(jnp.bfloat16)
        score_grad = lax.optimization_barrier(score_grad).astype(jnp.float32)
        query_grad = jnp.einsum('hqk,khd->qhd', score_grad, keys_wide)
        key_grad = key_grad + jnp.einsum('hqk,qhd->khd', score_grad, query_block)
        return ((key_grad, value_grad), query_grad)
    zeros_grad = jnp.zeros((token_total, head_total, HD), jnp.float32)
    block_ids = jnp.arange(token_total // block_rows, dtype=jnp.int32)
    (key_grad, value_grad), query_grad = lax.scan(one_block, (zeros_grad, zeros_grad), (block_ids, log_total))
    return (query_grad.reshape(token_total, head_total, HD), key_grad, value_grad)

def layer_forward(residual, gain_pair, bias_pair, qkv_weight, out_weight, up_weight, down_weight, segment, is_valid, cosine_table, sine_table):
    mean_value = lax.optimization_barrier(jnp.mean(residual, axis=1, keepdims=True))
    var_value = lax.optimization_barrier(jnp.mean(residual * residual, axis=1, keepdims=True)) - mean_value * mean_value
    inv_std = lax.rsqrt(var_value + EPSILON)
    normed = (residual - mean_value) * inv_std
    attn_in = (normed * gain_pair[0] + bias_pair[0]).astype(jnp.bfloat16)
    mlp_in = (normed * gain_pair[1] + bias_pair[1]).astype(jnp.bfloat16)
    projected = jnp.dot(attn_in, qkv_weight, preferred_element_type=jnp.float32)
    pre_act = jnp.dot(mlp_in, up_weight, preferred_element_type=jnp.float32)
    packed = rotary_pack(projected, cosine_table, sine_table)
    hidden = gelu_exact(pre_act).astype(jnp.bfloat16)
    queries, key_rows, values = split_heads(packed)
    attended, log_total = attend_forward(queries, key_rows, values, segment, is_valid)
    attended_flat = attended.reshape(attended.shape[0], -1)
    attn_branch = jnp.dot(attended_flat, out_weight, preferred_element_type=jnp.float32)
    mlp_branch = jnp.dot(hidden, down_weight, preferred_element_type=jnp.float32)
    result = residual + attn_branch + mlp_branch
    saved_state = (normed, inv_std, attn_in, mlp_in, pre_act, queries, key_rows, values, attended_flat, log_total, hidden)
    return (result, saved_state)

def layer_backward(grad_state, saved_state, gain_pair, qkv_weight, out_weight, up_weight, down_weight, segment, is_valid, cosine_table, sine_table):
    normed, inv_std, attn_in, mlp_in, pre_act, queries, key_rows, values, attended_flat, log_total, hidden = saved_state
    row_total = attended_flat.shape[0]
    head_total = queries.shape[1]
    grad_low = grad_state.astype(jnp.bfloat16)
    grad_out_weight = jnp.dot(attended_flat.T, grad_low, preferred_element_type=jnp.float32)
    grad_down_weight = jnp.dot(hidden.T, grad_low, preferred_element_type=jnp.float32)
    grad_att = jnp.dot(grad_low, out_weight.T, preferred_element_type=jnp.float32).astype(jnp.bfloat16)
    grad_hidden = jnp.dot(grad_low, down_weight.T, preferred_element_type=jnp.float32)
    grad_pre = (grad_hidden * gelu_slope(pre_act)).astype(jnp.bfloat16)
    query_grad, key_grad, value_grad = attend_backward(queries, key_rows, values, attended_flat.reshape(row_total, head_total, HD), grad_att.reshape(row_total, head_total, HD), log_total, segment, is_valid)
    query_grad = rotate_pairs(query_grad, cosine_table, sine_table, -1.0)
    key_grad = rotate_pairs(key_grad, cosine_table, sine_table, -1.0)
    grad_proj = jnp.stack([query_grad, key_grad, value_grad], axis=2).reshape(row_total, -1).astype(jnp.bfloat16)
    grad_qkv_weight = jnp.dot(attn_in.T, grad_proj, preferred_element_type=jnp.float32)
    grad_up_weight = jnp.dot(mlp_in.T, grad_pre, preferred_element_type=jnp.float32)
    grad_attn_in = jnp.dot(grad_proj, qkv_weight.T, preferred_element_type=jnp.float32)
    grad_mlp_in = jnp.dot(grad_pre, up_weight.T, preferred_element_type=jnp.float32)
    gain_grad = jnp.stack([lax.optimization_barrier(jnp.sum(grad_attn_in * normed, axis=0)), lax.optimization_barrier(jnp.sum(grad_mlp_in * normed, axis=0))])
    bias_grad = jnp.stack([lax.optimization_barrier(jnp.sum(grad_attn_in, axis=0)), lax.optimization_barrier(jnp.sum(grad_mlp_in, axis=0))])
    grad_normed = grad_attn_in * gain_pair[0] + grad_mlp_in * gain_pair[1]
    plain_mean = lax.optimization_barrier(jnp.mean(grad_normed, axis=1, keepdims=True))
    cross_mean = lax.optimization_barrier(jnp.mean(grad_normed * normed, axis=1, keepdims=True))
    grad_before = grad_state + inv_std * (grad_normed - plain_mean - normed * cross_mean)
    weight_grads = (grad_qkv_weight, grad_out_weight, grad_up_weight, grad_down_weight)
    return (grad_before, weight_grads, gain_grad, bias_grad)

def reference(block_input, seq_lens, seq_offsets, ln_gain, ln_bias, w_qkv, w_attn_out, w_up, w_down, cotangent):
    shard_total = seq_lens.shape[0]
    inputs_by_shard = block_input.reshape(shard_total, TOK_DP, D)
    cots_by_shard = cotangent.reshape(shard_total, TOK_DP, D)

    def one_shard(running, shard_inputs):
        residual, grad_state, lengths, offsets = shard_inputs
        segment, position, is_valid = token_layout(lengths, offsets, TOK_DP)
        cosine_table, sine_table = rotary_tables(position)
        saved_list = []
        for layer_index in range(LAYERS):
            residual, saved_state = layer_forward(residual, ln_gain[layer_index], ln_bias[layer_index], w_qkv[layer_index], w_attn_out[layer_index], w_up[layer_index], w_down[layer_index], segment, is_valid, cosine_table, sine_table)
            saved_list.append(saved_state)
        weight_list = [None] * LAYERS
        gain_list = [None] * LAYERS
        bias_list = [None] * LAYERS
        for layer_index in reversed(range(LAYERS)):
            grad_state, weight_grads, gain_grad, bias_grad = layer_backward(grad_state, saved_list[layer_index], ln_gain[layer_index], w_qkv[layer_index], w_attn_out[layer_index], w_up[layer_index], w_down[layer_index], segment, is_valid, cosine_table, sine_table)
            weight_list[layer_index] = weight_grads
            gain_list[layer_index] = gain_grad
            bias_list[layer_index] = bias_grad
        stacked = (jnp.stack(gain_list), jnp.stack(bias_list), jnp.stack([entry_grads[0] for entry_grads in weight_list]), jnp.stack([entry_grads[1] for entry_grads in weight_list]), jnp.stack([entry_grads[2] for entry_grads in weight_list]), jnp.stack([entry_grads[3] for entry_grads in weight_list]))
        updated = tuple((earlier + latest for earlier, latest in zip(running, stacked)))
        return (updated, (residual, grad_state))
    initial = (jnp.zeros((LAYERS, 2, D), jnp.float32), jnp.zeros((LAYERS, 2, D), jnp.float32), jnp.zeros((LAYERS, D, 3 * D), jnp.float32), jnp.zeros((LAYERS, D, D), jnp.float32), jnp.zeros((LAYERS, D, FF), jnp.float32), jnp.zeros((LAYERS, FF, D), jnp.float32))
    totals, (outputs, grads) = lax.scan(one_shard, initial, (inputs_by_shard, cots_by_shard, seq_lens, seq_offsets))
    block_output = outputs.reshape(shard_total * TOK_DP, D)
    grad_input = grads.reshape(shard_total * TOK_DP, D)
    return (block_output, grad_input, totals[0], totals[1], totals[2], totals[3], totals[4], totals[5])
```

```python
import math

import functools

import jax
import jax.numpy as jnp
from jax import lax
from jax.experimental import pallas as pl
from jax.experimental.pallas import tpu as pltpu
from jax.sharding import PartitionSpec as P

D = 768
HD = 64
ROT = 16
LAYERS = 2
BLOCK = 128


EPSILON = 1e-05
NEG_LARGE = -1e30


def token_layout(lengths, offsets, token_total):
    tokens = jnp.arange(token_total, dtype=jnp.int32)
    block_of = tokens // BLOCK
    slot_ids = jnp.arange(lengths.shape[0], dtype=jnp.int32)
    begun_flags = (offsets[None, :] <= block_of[:, None]).astype(jnp.int32)
    segment = jnp.sum(begun_flags, axis=1) - 1
    picked = (slot_ids[None, :] == segment[:, None]).astype(jnp.int32)
    first_block = jnp.sum(picked * offsets[None, :], axis=1)
    seq_length = jnp.sum(picked * lengths[None, :], axis=1)
    position = tokens - first_block * BLOCK
    return (segment, position, position < seq_length)


def rotary_tables(position):
    half_rot = ROT // 2
    frequency = jnp.exp(jnp.arange(half_rot, dtype=jnp.float32) * (-2.0 * math.log(10000.0) / ROT))
    angles = position.astype(jnp.float32)[:, None] * frequency[None, :]
    return (jnp.cos(angles), jnp.sin(angles))


def rotate_pairs(head_values, cosine_table, sine_table, direction):
    half_rot = ROT // 2
    lead_half = head_values[..., :half_rot]
    next_half = head_values[..., half_rot:ROT]
    tail_dims = head_values[..., ROT:]
    cos_wide = cosine_table[:, None, :]
    sin_wide = sine_table[:, None, :] * direction
    return jnp.concatenate(
        [
            lead_half * cos_wide - next_half * sin_wide,
            next_half * cos_wide + lead_half * sin_wide,
            tail_dims,
        ],
        axis=-1,
    )


def rotary_pack(projected, cosine_table, sine_table):
    row_total = projected.shape[0]
    head_total = projected.shape[1] // (3 * HD)
    head_grid = projected.reshape(row_total, head_total, 3, HD)
    turned_q = rotate_pairs(head_grid[:, :, 0], cosine_table, sine_table, 1.0)
    turned_k = rotate_pairs(head_grid[:, :, 1], cosine_table, sine_table, 1.0)
    head_grid = jnp.stack([turned_q, turned_k, head_grid[:, :, 2]], axis=2)
    return head_grid.reshape(row_total, -1).astype(jnp.bfloat16)


def split_heads(packed):
    row_total = packed.shape[0]
    head_total = packed.shape[1] // (3 * HD)
    head_grid = packed.reshape(row_total, head_total, 3, HD)
    return (head_grid[:, :, 0], head_grid[:, :, 1], head_grid[:, :, 2])


def gelu_exact(pre_value):
    return 0.5 * pre_value * (1.0 + jax.scipy.special.erf(pre_value / math.sqrt(2.0)))


def gelu_slope(pre_value):
    cumulative = 0.5 * (1.0 + jax.scipy.special.erf(pre_value / math.sqrt(2.0)))
    return cumulative + pre_value * jnp.exp(-0.5 * pre_value * pre_value) / math.sqrt(2.0 * math.pi)


def allowed_block(row_start, row_count, segment, is_valid):
    row_ids = row_start + jnp.arange(row_count, dtype=jnp.int32)
    columns = jnp.arange(segment.shape[0], dtype=jnp.int32)
    inside = (
        (segment[:, None] == segment[None, :])
        & (columns[None, :] <= row_ids[:, None])
        & is_valid[None, :]
    )
    return inside | (columns[None, :] == row_ids[:, None])


def attend_forward(queries, key_rows, values, segment, is_valid):
    token_total = queries.shape[0]
    head_total = queries.shape[1]
    score_scale = 1.0 / math.sqrt(HD)

    def one_block(block_index):
        row_start = block_index * token_total
        scores = (
            jnp.einsum("qhd,khd->hqk", queries, key_rows, preferred_element_type=jnp.float32)
            * score_scale
        )
        allowed = allowed_block(row_start, token_total, segment, is_valid)
        scores = jnp.where(allowed[None], scores, NEG_LARGE)
        top_score = jnp.max(scores, axis=2, keepdims=True)
        log_total = top_score + jnp.log(jnp.sum(jnp.exp(scores - top_score), axis=2, keepdims=True))
        prob_low = jnp.exp(scores - log_total).astype(jnp.bfloat16)
        attended = jnp.einsum("hqk,khd->qhd", prob_low, values, preferred_element_type=jnp.float32)
        return (attended.astype(jnp.bfloat16), log_total[:, :, 0])

    block_ids = jnp.arange(token_total // token_total, dtype=jnp.int32)
    attended, log_total = lax.map(one_block, block_ids)
    return (attended.reshape(token_total, head_total, HD), log_total)


def attend_backward(queries, key_rows, values, attended, grad_att, log_total, segment, is_valid):
    token_total = queries.shape[0]
    head_total = queries.shape[1]
    score_scale = 1.0 / math.sqrt(HD)

    def one_block(running, block_inputs):
        key_grad, value_grad = running
        block_index, block_log = block_inputs
        row_start = block_index * token_total
        scores = (
            jnp.einsum("qhd,khd->hqk", queries, key_rows, preferred_element_type=jnp.float32)
            * score_scale
        )
        allowed = allowed_block(row_start, token_total, segment, is_valid)
        scores = jnp.where(allowed[None], scores, NEG_LARGE)
        prob_table = jnp.exp(scores - block_log[:, :, None])
        prob_low = prob_table.astype(jnp.bfloat16)
        value_grad = value_grad + jnp.einsum(
            "hqk,qhd->khd", prob_low, grad_att, preferred_element_type=jnp.float32
        )
        weight_grad = jnp.einsum(
            "qhd,khd->hqk", grad_att, values, preferred_element_type=jnp.float32
        )
        row_delta = jnp.transpose(
            jnp.sum(grad_att.astype(jnp.float32) * attended.astype(jnp.float32), axis=2)
        )
        score_grad = (prob_table * (weight_grad - row_delta[:, :, None]) * score_scale).astype(
            jnp.bfloat16
        )
        query_grad = jnp.einsum(
            "hqk,khd->qhd", score_grad, key_rows, preferred_element_type=jnp.float32
        )
        key_grad = key_grad + jnp.einsum(
            "hqk,qhd->khd", score_grad, queries, preferred_element_type=jnp.float32
        )
        return ((key_grad, value_grad), query_grad)

    zeros_grad = jnp.zeros((token_total, head_total, HD), jnp.float32)
    block_ids = jnp.arange(token_total // token_total, dtype=jnp.int32)
    (key_grad, value_grad), query_grad = lax.scan(
        one_block, (zeros_grad, zeros_grad), (block_ids, log_total)
    )
    return (query_grad.reshape(token_total, head_total, HD), key_grad, value_grad)


MESH = pl.DeviceIdType.MESH
VMEM_SPEC = pl.BlockSpec(memory_space=pltpu.VMEM)


def remote(src, dst, send_sem, recv_sem, target):
    return pltpu.make_async_remote_copy(
        src_ref=src, dst_ref=dst, send_sem=send_sem, recv_sem=recv_sem, device_id=target, device_id_type=MESH
    )


def greet(targets):
    barrier = pltpu.get_barrier_semaphore()
    for target in targets:
        pl.semaphore_signal(barrier, inc=1, device_id=target, device_id_type=MESH)
    pl.semaphore_wait(barrier, len(targets))


def row_exchange_kernel(kinds, n, *refs):
    count = len(kinds)
    ins, outs = refs[:count], refs[count : 2 * count]
    send, recv, own = refs[2 * count :]
    me = lax.axis_index("row")
    greet([{"row": lax.rem(me + d, n)} for d in range(1, n)])
    copies = []
    for i, kind in enumerate(kinds):
        for d in range(1, n):
            peer = lax.rem(me + d, n)
            piece = ins[i] if kind == "gather" else ins[i].at[peer]
            copy = remote(piece, outs[i].at[me], send.at[i, d - 1], recv.at[i, d - 1], {"row": peer})
            copy.start()
            copies.append(copy)
    for i, kind in enumerate(kinds):
        piece = ins[i] if kind == "gather" else ins[i].at[me]
        copy = pltpu.make_async_copy(piece, outs[i].at[me], own.at[i])
        copy.start()
        copies.append(copy)
    for copy in copies:
        copy.wait()


def row_exchange(kinds, arrays, collective_id):
    n = lax.axis_size("row")
    count = len(arrays)
    shapes = [(n,) + a.shape if k == "gather" else a.shape for k, a in zip(kinds, arrays)]
    return pl.pallas_call(
        functools.partial(row_exchange_kernel, kinds, n),
        out_shape=[jax.ShapeDtypeStruct(s, a.dtype) for s, a in zip(shapes, arrays)],
        in_specs=[VMEM_SPEC] * count,
        out_specs=[VMEM_SPEC] * count,
        scratch_shapes=[
            pltpu.SemaphoreType.DMA((count, n - 1)),
            pltpu.SemaphoreType.DMA((count, n - 1)),
            pltpu.SemaphoreType.DMA((count,)),
        ],
        compiler_params=pltpu.CompilerParams(collective_id=collective_id, has_side_effects=True),
    )(*arrays)


def group_places(n):
    r, c = lax.axis_index("row"), lax.axis_index("col")
    partner = c + 1 - 2 * lax.rem(c, 2)
    across = lax.rem(c + 2, 4)
    greet([{"row": lax.rem(r + d, n)} for d in range(1, n)] + [{"col": partner}, {"col": across}])
    return r, c, partner, across


def gather_kernel(n, x_ref, o_ref, own, zs, zr, ps, pr, ys, yr, fs, fr):
    r, c, partner, across = group_places(n)
    started = []
    mine = pltpu.make_async_copy(x_ref, o_ref.at[c, r], own)
    mine.start()
    hops = []
    for d in range(1, n):
        hop = remote(x_ref, o_ref.at[c, r], zs.at[d - 1], zr.at[d - 1], {"row": lax.rem(r + d, n)})
        hop.start()
        hops.append(hop)
    nears, fars = [], []
    for k in range(n):
        rk = lax.rem(r + n - k, n)
        if k:
            hops[k - 1].wait_recv()
        block = o_ref.at[c, rk] if k else x_ref
        far = remote(block, o_ref.at[c, rk], ys.at[k], yr.at[k], {"col": across})
        far.start()
        near = remote(block, o_ref.at[c, rk], ps.at[k], pr.at[k], {"col": partner})
        near.start()
        fars.append(far)
        nears.append(near)
    passed = []
    for k in range(n):
        rk = lax.rem(r + n - k, n)
        fars[k].wait_recv()
        on = remote(o_ref.at[across, rk], o_ref.at[across, rk], fs.at[k], fr.at[k], {"col": partner})
        on.start()
        passed.append(on)
    for copy in nears + passed:
        copy.wait_recv()
    for copy in hops + fars + nears + passed:
        copy.wait_send()
    mine.wait()


def gather_tokens(x, collective_id):
    n = lax.axis_size("row")
    return pl.pallas_call(
        functools.partial(gather_kernel, n),
        out_shape=jax.ShapeDtypeStruct((4, n) + x.shape, x.dtype),
        in_specs=[VMEM_SPEC],
        out_specs=VMEM_SPEC,
        scratch_shapes=[pltpu.SemaphoreType.DMA]
        + [pltpu.SemaphoreType.DMA((n - 1,))] * 2
        + [pltpu.SemaphoreType.DMA((n,))] * 6,
        compiler_params=pltpu.CompilerParams(collective_id=collective_id, has_side_effects=True),
    )(x)


def reduce_kernel(n, p_ref, o_ref, a_buf, b_out, b_in, c_out, c_in, a_s, a_r, b_s, b_r, c_s, c_r):
    r, c, partner, across = group_places(n)
    beyond = lax.rem(partner + 2, 4)
    firsts = []
    for slot, dest in ((1, beyond), (0, partner)):
        copy = remote(p_ref.at[dest], a_buf.at[slot], a_s.at[slot], a_r.at[slot], {"col": partner})
        copy.start()
        firsts.append(copy)
    order = list(range(1, n)) + [0]
    seconds = {}
    firsts[0].wait_recv()
    for d in order:
        k = lax.rem(r + d, n)
        b_out[d] = (p_ref[across, k].astype(jnp.float32) + a_buf[1, k].astype(jnp.float32)).astype(jnp.bfloat16)
        copy = remote(b_out.at[d], b_in.at[d], b_s.at[d], b_r.at[d], {"col": across})
        copy.start()
        seconds[d] = copy
    firsts[1].wait_recv()
    thirds = []
    total = None
    for d in order:
        k = lax.rem(r + d, n)
        seconds[d].wait_recv()
        total = p_ref[c, k].astype(jnp.float32) + a_buf[0, k].astype(jnp.float32) + b_in[d].astype(jnp.float32)
        if d:
            c_out[d - 1] = total.astype(jnp.bfloat16)
            copy = remote(c_out.at[d - 1], c_in.at[d - 1], c_s.at[d - 1], c_r.at[d - 1], {"row": k})
            copy.start()
            thirds.append(copy)
    o_ref[...] = total
    for d, copy in enumerate(thirds):
        copy.wait_recv()
        o_ref[...] += c_in[d].astype(jnp.float32)
    for copy in firsts + list(seconds.values()) + thirds:
        copy.wait_send()


def reduce_tokens(p, collective_id):
    n = lax.axis_size("row")
    block = p.shape[2:]
    low = jnp.bfloat16
    return pl.pallas_call(
        functools.partial(reduce_kernel, n),
        out_shape=jax.ShapeDtypeStruct(block, jnp.float32),
        in_specs=[VMEM_SPEC],
        out_specs=VMEM_SPEC,
        scratch_shapes=[
            pltpu.VMEM((2, n) + block, low),
            pltpu.VMEM((n,) + block, low),
            pltpu.VMEM((n,) + block, low),
            pltpu.VMEM((n - 1,) + block, low),
            pltpu.VMEM((n - 1,) + block, low),
            pltpu.SemaphoreType.DMA((2,)),
            pltpu.SemaphoreType.DMA((2,)),
            pltpu.SemaphoreType.DMA((n,)),
            pltpu.SemaphoreType.DMA((n,)),
            pltpu.SemaphoreType.DMA((n - 1,)),
            pltpu.SemaphoreType.DMA((n - 1,)),
        ],
        compiler_params=pltpu.CompilerParams(collective_id=collective_id, has_side_effects=True),
    )(p)


def shift_exchange(kind, array):
    n = lax.axis_size("row")
    me = lax.axis_index("row")
    got = []
    for d in range(n):
        if kind == "gather":
            piece = array
        else:
            piece = lax.dynamic_index_in_dim(array, lax.rem(me + d, n), 0, keepdims=False)
        if d:
            piece = lax.ppermute(piece, "row", [(i, (i + d) % n) for i in range(n)])
        got.append(piece)
    stacked = jnp.stack(got)
    return jnp.take(stacked, lax.rem(me + n - jnp.arange(n), n), axis=0)


def columns_first(matrix, n):
    return matrix.reshape(matrix.shape[0], n, -1).transpose(1, 0, 2)


def columns_last(pieces):
    return pieces.transpose(1, 0, 2).reshape(pieces.shape[1], -1)


def local(
    block_input, seq_lens, seq_offsets, ln_gain, ln_bias, w_qkv, w_attn_out, w_up, w_down, cotangent
):
    n = lax.axis_size("row")
    row = lax.axis_index("row")
    part = block_input.shape[1]
    held = block_input.shape[0] // n
    shard_tokens = block_input.shape[0] * lax.axis_size("col")
    segment, position, is_valid = token_layout(seq_lens[0], seq_offsets[0], shard_tokens)
    cosine_table, sine_table = rotary_tables(position)
    token_row = (jnp.arange(shard_tokens, dtype=jnp.int32) // held) % n
    is_mine = (token_row == row)[:, None]
    zero_low = jnp.zeros((), jnp.bfloat16)

    def weight_pieces(l):
        return [
            w_qkv[l],
            w_attn_out[l],
            columns_first(w_up[l], n),
            w_down[l].reshape(n, -1, part),
        ]

    def whole_weights(qkv, out, up, down):
        return (qkv.reshape(n * part, -1), columns_last(out), up.reshape(n * part, -1), columns_last(down))

    norms = jnp.concatenate([ln_gain.reshape(-1, part), ln_bias.reshape(-1, part)], axis=0)
    weight_kinds = ("gather", "gather", "swap", "swap")
    got = row_exchange(
        ("swap", "swap", "gather") + weight_kinds,
        [block_input.reshape(n, held, part), cotangent.reshape(n, held, part), norms] + weight_pieces(0),
        0,
    )
    residual = columns_last(got[0])
    grad_state = columns_last(got[1])
    norms = columns_last(got[2]).reshape(2, LAYERS, 2, -1)
    weights = [whole_weights(*got[3:])]
    later = [shift_exchange(k, a) for k, a in zip(weight_kinds, weight_pieces(1))]
    weights.append(whole_weights(*later))
    gains, biases = norms[0], norms[1]

    saved = []
    grad_all = None
    for l in range(LAYERS):
        qkv_w, out_w, up_w, down_w = weights[l]
        mean = jnp.mean(residual, axis=1, keepdims=True)
        inv_std = lax.rsqrt(jnp.mean(residual * residual, axis=1, keepdims=True) - mean * mean + EPSILON)
        normed = (residual - mean) * inv_std
        normed_low = normed.astype(jnp.bfloat16)
        if l == 0:
            both = gather_tokens(jnp.stack([normed_low, grad_state.astype(jnp.bfloat16)]), 1)
            all_normed = both[:, :, 0].reshape(shard_tokens, -1)
            grad_all = both[:, :, 1].reshape(shard_tokens, -1)
        else:
            all_normed = gather_tokens(normed_low, 2).reshape(shard_tokens, -1)
        wide = all_normed.astype(jnp.float32)
        attn_in = (wide * gains[l, 0] + biases[l, 0]).astype(jnp.bfloat16)
        mlp_in = (wide * gains[l, 1] + biases[l, 1]).astype(jnp.bfloat16)
        proj = jnp.dot(attn_in, qkv_w, preferred_element_type=jnp.float32)
        pre = jnp.dot(mlp_in, up_w, preferred_element_type=jnp.float32)
        packed = rotary_pack(proj, cosine_table, sine_table)
        hidden = gelu_exact(pre).astype(jnp.bfloat16)
        queries, key_rows, values = split_heads(packed)
        attended, log_total = attend_forward(queries, key_rows, values, segment, is_valid)
        attended_flat = attended.reshape(shard_tokens, -1)
        branch = jnp.dot(
            jnp.where(is_mine, attended_flat, zero_low), out_w, preferred_element_type=jnp.float32
        ) + jnp.dot(hidden, down_w, preferred_element_type=jnp.float32)
        branch = branch.astype(jnp.bfloat16).reshape(-1, n, held, n * part)
        saved.append(
            (normed, inv_std, wide, attn_in, mlp_in, pre, queries, key_rows, values, attended_flat, log_total, hidden)
        )
        residual = residual + reduce_tokens(branch, 3)
    output = columns_first(residual, n)
    output = shift_exchange("swap", output).reshape(-1, part)

    weight_list = [None] * LAYERS
    vector_list = [None] * LAYERS
    for l in reversed(range(LAYERS)):
        (normed, inv_std, wide, attn_in, mlp_in, pre, queries, key_rows, values, attended_flat, log_total, hidden) = saved[l]
        qkv_w, out_w, up_w, down_w = weights[l]
        heads = queries.shape[1]
        if l < LAYERS - 1:
            grad_all = gather_tokens(grad_state.astype(jnp.bfloat16), 2).reshape(shard_tokens, -1)
        my_grad = lax.dynamic_slice_in_dim(grad_all, row * part, part, 1)
        grad_out_w = jnp.dot(attended_flat.T, my_grad, preferred_element_type=jnp.float32)
        grad_down_w = jnp.dot(hidden.T, grad_all, preferred_element_type=jnp.float32)
        grad_att = jnp.dot(grad_all, out_w.T, preferred_element_type=jnp.float32).astype(jnp.bfloat16)
        grad_hidden = jnp.dot(grad_all, down_w.T, preferred_element_type=jnp.float32)
        grad_pre = (grad_hidden * gelu_slope(pre)).astype(jnp.bfloat16)
        query_grad, key_grad, value_grad = attend_backward(
            queries,
            key_rows,
            values,
            attended_flat.reshape(shard_tokens, heads, HD),
            grad_att.reshape(shard_tokens, heads, HD),
            log_total,
            segment,
            is_valid,
        )
        query_grad = rotate_pairs(query_grad, cosine_table, sine_table, -1.0)
        key_grad = rotate_pairs(key_grad, cosine_table, sine_table, -1.0)
        grad_proj = (
            jnp.stack([query_grad, key_grad, value_grad], axis=2).reshape(shard_tokens, -1).astype(jnp.bfloat16)
        )
        my_attn_in = lax.dynamic_slice_in_dim(attn_in, row * part, part, 1)
        grad_qkv_w = jnp.dot(my_attn_in.T, grad_proj, preferred_element_type=jnp.float32)
        grad_up_w = jnp.dot(mlp_in.T, grad_pre, preferred_element_type=jnp.float32)
        grad_attn_in = jnp.dot(
            jnp.where(is_mine, grad_proj, zero_low), qkv_w.T, preferred_element_type=jnp.float32
        )
        grad_mlp_in = jnp.dot(grad_pre, up_w.T, preferred_element_type=jnp.float32)
        vector_list[l] = jnp.stack(
            [
                jnp.sum(grad_attn_in * wide, axis=0),
                jnp.sum(grad_mlp_in * wide, axis=0),
                jnp.sum(grad_attn_in, axis=0),
                jnp.sum(grad_mlp_in, axis=0),
            ]
        )
        mixed = (grad_attn_in * gains[l, 0] + grad_mlp_in * gains[l, 1]).astype(jnp.bfloat16)
        grad_normed = reduce_tokens(mixed.reshape(-1, n, held, n * part), 3)
        plain_mean = jnp.mean(grad_normed, axis=1, keepdims=True)
        cross_mean = jnp.mean(grad_normed * normed, axis=1, keepdims=True)
        grad_state = grad_state + inv_std * (grad_normed - plain_mean - normed * cross_mean)
        down_pieces = columns_first(grad_down_w.astype(jnp.bfloat16), n)
        up_pieces = grad_up_w.astype(jnp.bfloat16).reshape(n, part, -1)
        if l:
            down_mine = shift_exchange("swap", down_pieces)
            up_mine = shift_exchange("swap", up_pieces)
        else:
            down_mine, up_mine, final_grad = row_exchange(
                ("swap",) * 3, [down_pieces, up_pieces, columns_first(grad_state, n)], 4
            )
        weight_list[l] = lax.psum(
            (
                grad_qkv_w.astype(jnp.bfloat16),
                grad_out_w.astype(jnp.bfloat16),
                columns_last(up_mine),
                down_mine.reshape(-1, part),
            ),
            "dp",
        )
    totals = [jnp.stack([w[i] for w in weight_list]).astype(jnp.float32) for i in range(4)]
    vectors = lax.psum(jnp.stack(vector_list), ("dp", "row", "col"))
    vectors = lax.dynamic_slice_in_dim(vectors, row * part, part, 2)
    return (output, final_grad.reshape(-1, part), vectors[:, :2], vectors[:, 2:], *totals)


def solution(mesh):
    return jax.shard_map(
        local,
        mesh=mesh,
        in_specs=(
            P(("dp", "col"), "row"),
            P("dp", None),
            P("dp", None),
            P(None, None, "row"),
            P(None, None, "row"),
            P(None, "row", "col"),
            P(None, "col", "row"),
            P(None, "row", "col"),
            P(None, "col", "row"),
            P(("dp", "col"), "row"),
        ),
        out_specs=(
            P(("dp", "col"), "row"),
            P(("dp", "col"), "row"),
            P(None, None, "row"),
            P(None, None, "row"),
            P(None, "row", "col"),
            P(None, "col", "row"),
            P(None, "row", "col"),
            P(None, "col", "row"),
        ),
        check_vma=False,
    )
```

```python
import math

import functools

import jax
import jax.numpy as jnp
from jax import lax
from jax.experimental import pallas as pl
from jax.experimental.pallas import tpu as pltpu
from jax.sharding import PartitionSpec as P

D = 768
HD = 64
ROT = 16
LAYERS = 2
BLOCK = 128


EPSILON = 1e-05
NEG_LARGE = -1e30


def token_layout(lengths, offsets, token_total):
    tokens = jnp.arange(token_total, dtype=jnp.int32)
    block_of = tokens // BLOCK
    slot_ids = jnp.arange(lengths.shape[0], dtype=jnp.int32)
    begun_flags = (offsets[None, :] <= block_of[:, None]).astype(jnp.int32)
    segment = jnp.sum(begun_flags, axis=1) - 1
    picked = (slot_ids[None, :] == segment[:, None]).astype(jnp.int32)
    first_block = jnp.sum(picked * offsets[None, :], axis=1)
    seq_length = jnp.sum(picked * lengths[None, :], axis=1)
    position = tokens - first_block * BLOCK
    return (segment, position, position < seq_length)


def rotary_tables(position):
    half_rot = ROT // 2
    frequency = jnp.exp(jnp.arange(half_rot, dtype=jnp.float32) * (-2.0 * math.log(10000.0) / ROT))
    angles = position.astype(jnp.float32)[:, None] * frequency[None, :]
    return (jnp.cos(angles), jnp.sin(angles))


def rotate_pairs(head_values, cosine_table, sine_table, direction):
    half_rot = ROT // 2
    lead_half = head_values[..., :half_rot]
    next_half = head_values[..., half_rot:ROT]
    tail_dims = head_values[..., ROT:]
    cos_wide = cosine_table[:, None, :]
    sin_wide = sine_table[:, None, :] * direction
    return jnp.concatenate(
        [
            lead_half * cos_wide - next_half * sin_wide,
            next_half * cos_wide + lead_half * sin_wide,
            tail_dims,
        ],
        axis=-1,
    )


def rotary_pack(projected, cosine_table, sine_table):
    row_total = projected.shape[0]
    head_total = projected.shape[1] // (3 * HD)
    head_grid = projected.reshape(row_total, head_total, 3, HD)
    turned_q = rotate_pairs(head_grid[:, :, 0], cosine_table, sine_table, 1.0)
    turned_k = rotate_pairs(head_grid[:, :, 1], cosine_table, sine_table, 1.0)
    head_grid = jnp.stack([turned_q, turned_k, head_grid[:, :, 2]], axis=2)
    return head_grid.reshape(row_total, -1).astype(jnp.bfloat16)


def split_heads(packed):
    row_total = packed.shape[0]
    head_total = packed.shape[1] // (3 * HD)
    head_grid = packed.reshape(row_total, head_total, 3, HD)
    return (head_grid[:, :, 0], head_grid[:, :, 1], head_grid[:, :, 2])


def gelu_exact(pre_value):
    return 0.5 * pre_value * (1.0 + jax.scipy.special.erf(pre_value / math.sqrt(2.0)))


def gelu_slope(pre_value):
    cumulative = 0.5 * (1.0 + jax.scipy.special.erf(pre_value / math.sqrt(2.0)))
    return cumulative + pre_value * jnp.exp(-0.5 * pre_value * pre_value) / math.sqrt(2.0 * math.pi)


def allowed_block(row_start, row_count, segment, is_valid):
    row_ids = row_start + jnp.arange(row_count, dtype=jnp.int32)
    columns = jnp.arange(segment.shape[0], dtype=jnp.int32)
    inside = (
        (segment[:, None] == segment[None, :])
        & (columns[None, :] <= row_ids[:, None])
        & is_valid[None, :]
    )
    return inside | (columns[None, :] == row_ids[:, None])


def attend_forward(queries, key_rows, values, segment, is_valid):
    token_total = queries.shape[0]
    head_total = queries.shape[1]
    score_scale = 1.0 / math.sqrt(HD)

    def one_block(block_index):
        row_start = block_index * token_total
        scores = (
            jnp.einsum("qhd,khd->hqk", queries, key_rows, preferred_element_type=jnp.float32)
            * score_scale
        )
        allowed = allowed_block(row_start, token_total, segment, is_valid)
        scores = jnp.where(allowed[None], scores, NEG_LARGE)
        top_score = jnp.max(scores, axis=2, keepdims=True)
        log_total = top_score + jnp.log(jnp.sum(jnp.exp(scores - top_score), axis=2, keepdims=True))
        prob_low = jnp.exp(scores - log_total).astype(jnp.bfloat16)
        attended = jnp.einsum("hqk,khd->qhd", prob_low, values, preferred_element_type=jnp.float32)
        return (attended.astype(jnp.bfloat16), log_total[:, :, 0])

    block_ids = jnp.arange(token_total // token_total, dtype=jnp.int32)
    attended, log_total = lax.map(one_block, block_ids)
    return (attended.reshape(token_total, head_total, HD), log_total)


def attend_backward(queries, key_rows, values, attended, grad_att, log_total, segment, is_valid):
    token_total = queries.shape[0]
    head_total = queries.shape[1]
    score_scale = 1.0 / math.sqrt(HD)

    def one_block(running, block_inputs):
        key_grad, value_grad = running
        block_index, block_log = block_inputs
        row_start = block_index * token_total
        scores = (
            jnp.einsum("qhd,khd->hqk", queries, key_rows, preferred_element_type=jnp.float32)
            * score_scale
        )
        allowed = allowed_block(row_start, token_total, segment, is_valid)
        scores = jnp.where(allowed[None], scores, NEG_LARGE)
        prob_table = jnp.exp(scores - block_log[:, :, None])
        prob_low = prob_table.astype(jnp.bfloat16)
        value_grad = value_grad + jnp.einsum(
            "hqk,qhd->khd", prob_low, grad_att, preferred_element_type=jnp.float32
        )
        weight_grad = jnp.einsum(
            "qhd,khd->hqk", grad_att, values, preferred_element_type=jnp.float32
        )
        row_delta = jnp.transpose(
            jnp.sum(grad_att.astype(jnp.float32) * attended.astype(jnp.float32), axis=2)
        )
        score_grad = (prob_table * (weight_grad - row_delta[:, :, None]) * score_scale).astype(
            jnp.bfloat16
        )
        query_grad = jnp.einsum(
            "hqk,khd->qhd", score_grad, key_rows, preferred_element_type=jnp.float32
        )
        key_grad = key_grad + jnp.einsum(
            "hqk,qhd->khd", score_grad, queries, preferred_element_type=jnp.float32
        )
        return ((key_grad, value_grad), query_grad)

    zeros_grad = jnp.zeros((token_total, head_total, HD), jnp.float32)
    block_ids = jnp.arange(token_total // token_total, dtype=jnp.int32)
    (key_grad, value_grad), query_grad = lax.scan(
        one_block, (zeros_grad, zeros_grad), (block_ids, log_total)
    )
    return (query_grad.reshape(token_total, head_total, HD), key_grad, value_grad)


MESH = pl.DeviceIdType.MESH
VMEM_SPEC = pl.BlockSpec(memory_space=pltpu.VMEM)


def remote(src, dst, send_sem, recv_sem, target):
    return pltpu.make_async_remote_copy(
        src_ref=src, dst_ref=dst, send_sem=send_sem, recv_sem=recv_sem, device_id=target, device_id_type=MESH
    )


def greet(targets):
    barrier = pltpu.get_barrier_semaphore()
    for target in targets:
        pl.semaphore_signal(barrier, inc=1, device_id=target, device_id_type=MESH)
    pl.semaphore_wait(barrier, len(targets))


def row_exchange_kernel(kinds, n, *refs):
    count = len(kinds)
    ins, outs = refs[:count], refs[count : 2 * count]
    send, recv, own = refs[2 * count :]
    me = lax.axis_index("row")
    greet([{"row": lax.rem(me + d, n)} for d in range(1, n)])
    copies = []
    for i, kind in enumerate(kinds):
        for d in range(1, n):
            peer = lax.rem(me + d, n)
            piece = ins[i] if kind == "gather" else ins[i].at[peer]
            copy = remote(piece, outs[i].at[me], send.at[i, d - 1], recv.at[i, d - 1], {"row": peer})
            copy.start()
            copies.append(copy)
    for i, kind in enumerate(kinds):
        piece = ins[i] if kind == "gather" else ins[i].at[me]
        copy = pltpu.make_async_copy(piece, outs[i].at[me], own.at[i])
        copy.start()
        copies.append(copy)
    for copy in copies:
        copy.wait()


def row_exchange(kinds, arrays, collective_id):
    n = lax.axis_size("row")
    count = len(arrays)
    shapes = [(n,) + a.shape if k == "gather" else a.shape for k, a in zip(kinds, arrays)]
    return pl.pallas_call(
        functools.partial(row_exchange_kernel, kinds, n),
        out_shape=[jax.ShapeDtypeStruct(s, a.dtype) for s, a in zip(shapes, arrays)],
        in_specs=[VMEM_SPEC] * count,
        out_specs=[VMEM_SPEC] * count,
        scratch_shapes=[
            pltpu.SemaphoreType.DMA((count, n - 1)),
            pltpu.SemaphoreType.DMA((count, n - 1)),
            pltpu.SemaphoreType.DMA((count,)),
        ],
        compiler_params=pltpu.CompilerParams(collective_id=collective_id, has_side_effects=True),
    )(*arrays)


def group_places(n):
    r, c = lax.axis_index("row"), lax.axis_index("col")
    partner = c + 1 - 2 * lax.rem(c, 2)
    across = lax.rem(c + 2, 4)
    greet([{"row": lax.rem(r + d, n)} for d in range(1, n)] + [{"col": partner}, {"col": across}])
    return r, c, partner, across


def gather_kernel(n, x_ref, o_ref, own, zs, zr, ps, pr, ys, yr, fs, fr):
    r, c, partner, across = group_places(n)
    started = []
    mine = pltpu.make_async_copy(x_ref, o_ref.at[c, r], own)
    mine.start()
    hops = []
    for d in range(1, n):
        hop = remote(x_ref, o_ref.at[c, r], zs.at[d - 1], zr.at[d - 1], {"row": lax.rem(r + d, n)})
        hop.start()
        hops.append(hop)
    nears, fars = [], []
    for k in range(n):
        rk = lax.rem(r + n - k, n)
        if k:
            hops[k - 1].wait_recv()
        block = o_ref.at[c, rk] if k else x_ref
        far = remote(block, o_ref.at[c, rk], ys.at[k], yr.at[k], {"col": across})
        far.start()
        near = remote(block, o_ref.at[c, rk], ps.at[k], pr.at[k], {"col": partner})
        near.start()
        fars.append(far)
        nears.append(near)
    passed = []
    for k in range(n):
        rk = lax.rem(r + n - k, n)
        fars[k].wait_recv()
        on = remote(o_ref.at[across, rk], o_ref.at[across, rk], fs.at[k], fr.at[k], {"col": partner})
        on.start()
        passed.append(on)
    for copy in nears + passed:
        copy.wait_recv()
    for copy in hops + fars + nears + passed:
        copy.wait_send()
    mine.wait()


def gather_tokens(x, collective_id):
    n = lax.axis_size("row")
    return pl.pallas_call(
        functools.partial(gather_kernel, n),
        out_shape=jax.ShapeDtypeStruct((4, n) + x.shape, x.dtype),
        in_specs=[VMEM_SPEC],
        out_specs=VMEM_SPEC,
        scratch_shapes=[pltpu.SemaphoreType.DMA]
        + [pltpu.SemaphoreType.DMA((n - 1,))] * 2
        + [pltpu.SemaphoreType.DMA((n,))] * 6,
        compiler_params=pltpu.CompilerParams(collective_id=collective_id, has_side_effects=True),
    )(x)


def reduce_kernel(n, p_ref, o_ref, a_buf, b_out, b_in, c_out, c_in, a_s, a_r, b_s, b_r, c_s, c_r):
    r, c, partner, across = group_places(n)
    beyond = lax.rem(partner + 2, 4)
    firsts = []
    for slot, dest in ((1, beyond), (0, partner)):
        copy = remote(p_ref.at[dest], a_buf.at[slot], a_s.at[slot], a_r.at[slot], {"col": partner})
        copy.start()
        firsts.append(copy)
    order = list(range(1, n)) + [0]
    seconds = {}
    firsts[0].wait_recv()
    for d in order:
        k = lax.rem(r + d, n)
        b_out[d] = (p_ref[across, k].astype(jnp.float32) + a_buf[1, k].astype(jnp.float32)).astype(jnp.bfloat16)
        copy = remote(b_out.at[d], b_in.at[d], b_s.at[d], b_r.at[d], {"col": across})
        copy.start()
        seconds[d] = copy
    firsts[1].wait_recv()
    thirds = []
    total = None
    for d in order:
        k = lax.rem(r + d, n)
        seconds[d].wait_recv()
        total = p_ref[c, k].astype(jnp.float32) + a_buf[0, k].astype(jnp.float32) + b_in[d].astype(jnp.float32)
        if d:
            c_out[d - 1] = total.astype(jnp.bfloat16)
            copy = remote(c_out.at[d - 1], c_in.at[d - 1], c_s.at[d - 1], c_r.at[d - 1], {"row": k})
            copy.start()
            thirds.append(copy)
    o_ref[...] = total
    for d, copy in enumerate(thirds):
        copy.wait_recv()
        o_ref[...] += c_in[d].astype(jnp.float32)
    for copy in firsts + list(seconds.values()) + thirds:
        copy.wait_send()


def reduce_tokens(p, collective_id):
    n = lax.axis_size("row")
    block = p.shape[2:]
    low = jnp.bfloat16
    return pl.pallas_call(
        functools.partial(reduce_kernel, n),
        out_shape=jax.ShapeDtypeStruct(block, jnp.float32),
        in_specs=[VMEM_SPEC],
        out_specs=VMEM_SPEC,
        scratch_shapes=[
            pltpu.VMEM((2, n) + block, low),
            pltpu.VMEM((n,) + block, low),
            pltpu.VMEM((n,) + block, low),
            pltpu.VMEM((n - 1,) + block, low),
            pltpu.VMEM((n - 1,) + block, low),
            pltpu.SemaphoreType.DMA((2,)),
            pltpu.SemaphoreType.DMA((2,)),
            pltpu.SemaphoreType.DMA((n,)),
            pltpu.SemaphoreType.DMA((n,)),
            pltpu.SemaphoreType.DMA((n - 1,)),
            pltpu.SemaphoreType.DMA((n - 1,)),
        ],
        compiler_params=pltpu.CompilerParams(collective_id=collective_id, has_side_effects=True),
    )(p)


def sum_shards(array):
    if lax.axis_size("dp") == 2:
        other = lax.ppermute(array, "dp", [(0, 1), (1, 0)])
        return array.astype(jnp.float32) + other.astype(jnp.float32)
    return lax.psum(array, "dp").astype(jnp.float32)


def columns_first(matrix, n):
    return matrix.reshape(matrix.shape[0], n, -1).transpose(1, 0, 2)


def columns_last(pieces):
    return pieces.transpose(1, 0, 2).reshape(pieces.shape[1], -1)


def local(
    block_input, seq_lens, seq_offsets, ln_gain, ln_bias, w_qkv, w_attn_out, w_up, w_down, cotangent
):
    n = lax.axis_size("row")
    row = lax.axis_index("row")
    part = block_input.shape[1]
    held = block_input.shape[0] // n
    shard_tokens = block_input.shape[0] * lax.axis_size("col")
    segment, position, is_valid = token_layout(seq_lens[0], seq_offsets[0], shard_tokens)
    cosine_table, sine_table = rotary_tables(position)
    token_row = (jnp.arange(shard_tokens, dtype=jnp.int32) // held) % n
    is_mine = (token_row == row)[:, None]
    zero_low = jnp.zeros((), jnp.bfloat16)

    def weight_pieces(l):
        return [
            jnp.concatenate([w_qkv[l], w_attn_out[l]], axis=1),
            jnp.concatenate([columns_first(w_up[l], n), w_down[l].reshape(n, -1, part)], axis=2),
        ]

    def whole_weights(gathered, swapped):
        wide_part = gathered.shape[2] - part
        return (
            gathered[:, :, :wide_part].reshape(n * part, wide_part),
            columns_last(gathered[:, :, wide_part:]),
            swapped[:, :, : swapped.shape[2] - part].reshape(n * part, -1),
            columns_last(swapped[:, :, swapped.shape[2] - part :]),
        )

    norms = jnp.concatenate([ln_gain.reshape(-1, part), ln_bias.reshape(-1, part)], axis=0)
    ends = jnp.concatenate([block_input.reshape(n, held, part), cotangent.reshape(n, held, part)], axis=2)
    got = row_exchange(
        ("swap", "gather") + ("gather", "swap") * LAYERS,
        [ends, norms] + [piece for l in range(LAYERS) for piece in weight_pieces(l)],
        0,
    )
    residual = columns_last(got[0][:, :, :part])
    grad_state = columns_last(got[0][:, :, part:])
    norms = columns_last(got[1]).reshape(2, LAYERS, 2, -1)
    weights = [whole_weights(*got[2 + 2 * l : 4 + 2 * l]) for l in range(LAYERS)]
    gains, biases = norms[0], norms[1]

    saved = []
    grad_all = None
    for l in range(LAYERS):
        qkv_w, out_w, up_w, down_w = weights[l]
        mean = jnp.mean(residual, axis=1, keepdims=True)
        inv_std = lax.rsqrt(jnp.mean(residual * residual, axis=1, keepdims=True) - mean * mean + EPSILON)
        normed = (residual - mean) * inv_std
        normed_low = normed.astype(jnp.bfloat16)
        if l == 0:
            both = gather_tokens(jnp.stack([normed_low, grad_state.astype(jnp.bfloat16)]), 1)
            all_normed = both[:, :, 0].reshape(shard_tokens, -1)
            grad_all = both[:, :, 1].reshape(shard_tokens, -1)
        else:
            all_normed = gather_tokens(normed_low, 2).reshape(shard_tokens, -1)
        wide = all_normed.astype(jnp.float32)
        attn_in = (wide * gains[l, 0] + biases[l, 0]).astype(jnp.bfloat16)
        mlp_in = (wide * gains[l, 1] + biases[l, 1]).astype(jnp.bfloat16)
        proj = jnp.dot(attn_in, qkv_w, preferred_element_type=jnp.float32)
        pre = jnp.dot(mlp_in, up_w, preferred_element_type=jnp.float32)
        packed = rotary_pack(proj, cosine_table, sine_table)
        hidden = gelu_exact(pre).astype(jnp.bfloat16)
        queries, key_rows, values = split_heads(packed)
        attended, log_total = attend_forward(queries, key_rows, values, segment, is_valid)
        attended_flat = attended.reshape(shard_tokens, -1)
        branch = jnp.dot(
            jnp.where(is_mine, attended_flat, zero_low), out_w, preferred_element_type=jnp.float32
        ) + jnp.dot(hidden, down_w, preferred_element_type=jnp.float32)
        branch = branch.astype(jnp.bfloat16).reshape(-1, n, held, n * part)
        saved.append(
            (normed, inv_std, wide, attn_in, mlp_in, pre, queries, key_rows, values, attended_flat, log_total, hidden)
        )
        residual = residual + reduce_tokens(branch, 3)
    swap_list = [None] * LAYERS
    weight_list = [None] * LAYERS
    vector_list = [None] * LAYERS
    for l in reversed(range(LAYERS)):
        (normed, inv_std, wide, attn_in, mlp_in, pre, queries, key_rows, values, attended_flat, log_total, hidden) = saved[l]
        qkv_w, out_w, up_w, down_w = weights[l]
        heads = queries.shape[1]
        if l < LAYERS - 1:
            grad_all = gather_tokens(grad_state.astype(jnp.bfloat16), 2).reshape(shard_tokens, -1)
        my_grad = lax.dynamic_slice_in_dim(grad_all, row * part, part, 1)
        grad_out_w = jnp.dot(attended_flat.T, my_grad, preferred_element_type=jnp.float32)
        grad_down_w = jnp.dot(hidden.T, grad_all, preferred_element_type=jnp.float32)
        grad_att = jnp.dot(grad_all, out_w.T, preferred_element_type=jnp.float32).astype(jnp.bfloat16)
        grad_hidden = jnp.dot(grad_all, down_w.T, preferred_element_type=jnp.float32)
        grad_pre = (grad_hidden * gelu_slope(pre)).astype(jnp.bfloat16)
        query_grad, key_grad, value_grad = attend_backward(
            queries,
            key_rows,
            values,
            attended_flat.reshape(shard_tokens, heads, HD),
            grad_att.reshape(shard_tokens, heads, HD),
            log_total,
            segment,
            is_valid,
        )
        query_grad = rotate_pairs(query_grad, cosine_table, sine_table, -1.0)
        key_grad = rotate_pairs(key_grad, cosine_table, sine_table, -1.0)
        grad_proj = (
            jnp.stack([query_grad, key_grad, value_grad], axis=2).reshape(shard_tokens, -1).astype(jnp.bfloat16)
        )
        my_attn_in = lax.dynamic_slice_in_dim(attn_in, row * part, part, 1)
        grad_qkv_w = jnp.dot(my_attn_in.T, grad_proj, preferred_element_type=jnp.float32)
        grad_up_w = jnp.dot(mlp_in.T, grad_pre, preferred_element_type=jnp.float32)
        grad_attn_in = jnp.dot(
            jnp.where(is_mine, grad_proj, zero_low), qkv_w.T, preferred_element_type=jnp.float32
        )
        grad_mlp_in = jnp.dot(grad_pre, up_w.T, preferred_element_type=jnp.float32)
        weight_list[l] = (
            sum_shards(grad_qkv_w.astype(jnp.bfloat16)),
            sum_shards(grad_out_w.astype(jnp.bfloat16)),
        )
        pieces = jnp.concatenate(
            [
                grad_up_w.astype(jnp.bfloat16).reshape(n, part, -1),
                columns_first(grad_down_w.astype(jnp.bfloat16), n),
            ],
            axis=2,
        )
        swap_list[l] = sum_shards(pieces).astype(jnp.bfloat16)
        vector_list[l] = jnp.stack(
            [
                jnp.sum(grad_attn_in * wide, axis=0),
                jnp.sum(grad_mlp_in * wide, axis=0),
                jnp.sum(grad_attn_in, axis=0),
                jnp.sum(grad_mlp_in, axis=0),
            ]
        )
        mixed = (grad_attn_in * gains[l, 0] + grad_mlp_in * gains[l, 1]).astype(jnp.bfloat16)
        grad_normed = reduce_tokens(mixed.reshape(-1, n, held, n * part), 3)
        plain_mean = jnp.mean(grad_normed, axis=1, keepdims=True)
        cross_mean = jnp.mean(grad_normed * normed, axis=1, keepdims=True)
        grad_state = grad_state + inv_std * (grad_normed - plain_mean - normed * cross_mean)
    ends = jnp.concatenate([columns_first(residual, n), columns_first(grad_state, n)], axis=2)
    got = row_exchange(("swap",) * (1 + LAYERS), [ends] + swap_list, 4)
    output = got[0][:, :, :part].reshape(-1, part)
    final_grad = got[0][:, :, part:].reshape(-1, part)
    totals = [
        jnp.stack([w[0] for w in weight_list]),
        jnp.stack([w[1] for w in weight_list]),
        jnp.stack([columns_last(g[:, :, : g.shape[2] - part]) for g in got[1:]]).astype(jnp.float32),
        jnp.stack([g[:, :, g.shape[2] - part :].reshape(-1, part) for g in got[1:]]).astype(jnp.float32),
    ]
    vectors = lax.psum(jnp.stack(vector_list), ("dp", "row", "col"))
    vectors = lax.dynamic_slice_in_dim(vectors, row * part, part, 2)
    return (output, final_grad, vectors[:, :2], vectors[:, 2:], *totals)


def solution(mesh):
    return jax.shard_map(
        local,
        mesh=mesh,
        in_specs=(
            P(("dp", "col"), "row"),
            P("dp", None),
            P("dp", None),
            P(None, None, "row"),
            P(None, None, "row"),
            P(None, "row", "col"),
            P(None, "col", "row"),
            P(None, "row", "col"),
            P(None, "col", "row"),
            P(("dp", "col"), "row"),
        ),
        out_specs=(
            P(("dp", "col"), "row"),
            P(("dp", "col"), "row"),
            P(None, None, "row"),
            P(None, None, "row"),
            P(None, "row", "col"),
            P(None, "col", "row"),
            P(None, "row", "col"),
            P(None, "col", "row"),
        ),
        check_vma=False,
    )
```

```python
import math

import functools

import jax
import jax.numpy as jnp
from jax import lax
from jax.experimental import pallas as pl
from jax.experimental.pallas import tpu as pltpu
from jax.sharding import PartitionSpec as P

D = 768
HD = 64
ROT = 16
LAYERS = 2
BLOCK = 128


EPSILON = 1e-05
NEG_LARGE = -1e30


def token_layout(lengths, offsets, token_total):
    tokens = jnp.arange(token_total, dtype=jnp.int32)
    block_of = tokens // BLOCK
    slot_ids = jnp.arange(lengths.shape[0], dtype=jnp.int32)
    begun_flags = (offsets[None, :] <= block_of[:, None]).astype(jnp.int32)
    segment = jnp.sum(begun_flags, axis=1) - 1
    picked = (slot_ids[None, :] == segment[:, None]).astype(jnp.int32)
    first_block = jnp.sum(picked * offsets[None, :], axis=1)
    seq_length = jnp.sum(picked * lengths[None, :], axis=1)
    position = tokens - first_block * BLOCK
    return (segment, position, position < seq_length)


def rotary_tables(position):
    half_rot = ROT // 2
    frequency = jnp.exp(jnp.arange(half_rot, dtype=jnp.float32) * (-2.0 * math.log(10000.0) / ROT))
    angles = position.astype(jnp.float32)[:, None] * frequency[None, :]
    return (jnp.cos(angles), jnp.sin(angles))


def rotate_pairs(head_values, cosine_table, sine_table, direction):
    half_rot = ROT // 2
    lead_half = head_values[..., :half_rot]
    next_half = head_values[..., half_rot:ROT]
    tail_dims = head_values[..., ROT:]
    cos_wide = cosine_table[:, None, :]
    sin_wide = sine_table[:, None, :] * direction
    return jnp.concatenate(
        [
            lead_half * cos_wide - next_half * sin_wide,
            next_half * cos_wide + lead_half * sin_wide,
            tail_dims,
        ],
        axis=-1,
    )


def rotary_pack(projected, cosine_table, sine_table):
    row_total = projected.shape[0]
    head_total = projected.shape[1] // (3 * HD)
    head_grid = projected.reshape(row_total, head_total, 3, HD)
    turned_q = rotate_pairs(head_grid[:, :, 0], cosine_table, sine_table, 1.0)
    turned_k = rotate_pairs(head_grid[:, :, 1], cosine_table, sine_table, 1.0)
    head_grid = jnp.stack([turned_q, turned_k, head_grid[:, :, 2]], axis=2)
    return head_grid.reshape(row_total, -1).astype(jnp.bfloat16)


def split_heads(packed):
    row_total = packed.shape[0]
    head_total = packed.shape[1] // (3 * HD)
    head_grid = packed.reshape(row_total, head_total, 3, HD)
    return (head_grid[:, :, 0], head_grid[:, :, 1], head_grid[:, :, 2])


def gelu_exact(pre_value):
    return 0.5 * pre_value * (1.0 + jax.scipy.special.erf(pre_value / math.sqrt(2.0)))


def gelu_slope(pre_value):
    cumulative = 0.5 * (1.0 + jax.scipy.special.erf(pre_value / math.sqrt(2.0)))
    return cumulative + pre_value * jnp.exp(-0.5 * pre_value * pre_value) / math.sqrt(2.0 * math.pi)


def allowed_block(row_start, row_count, segment, is_valid):
    row_ids = row_start + jnp.arange(row_count, dtype=jnp.int32)
    columns = jnp.arange(segment.shape[0], dtype=jnp.int32)
    inside = (
        (segment[:, None] == segment[None, :])
        & (columns[None, :] <= row_ids[:, None])
        & is_valid[None, :]
    )
    return inside | (columns[None, :] == row_ids[:, None])


def attend_forward(queries, key_rows, values, segment, is_valid):
    token_total = queries.shape[0]
    head_total = queries.shape[1]
    score_scale = 1.0 / math.sqrt(HD)

    def one_block(block_index):
        row_start = block_index * token_total
        scores = (
            jnp.einsum("qhd,khd->hqk", queries, key_rows, preferred_element_type=jnp.float32)
            * score_scale
        )
        allowed = allowed_block(row_start, token_total, segment, is_valid)
        scores = jnp.where(allowed[None], scores, NEG_LARGE)
        top_score = jnp.max(scores, axis=2, keepdims=True)
        log_total = top_score + jnp.log(jnp.sum(jnp.exp(scores - top_score), axis=2, keepdims=True))
        prob_low = jnp.exp(scores - log_total).astype(jnp.bfloat16)
        attended = jnp.einsum("hqk,khd->qhd", prob_low, values, preferred_element_type=jnp.float32)
        return (attended.astype(jnp.bfloat16), log_total[:, :, 0])

    block_ids = jnp.arange(token_total // token_total, dtype=jnp.int32)
    attended, log_total = lax.map(one_block, block_ids)
    return (attended.reshape(token_total, head_total, HD), log_total)


def attend_backward(queries, key_rows, values, attended, grad_att, log_total, segment, is_valid):
    token_total = queries.shape[0]
    head_total = queries.shape[1]
    score_scale = 1.0 / math.sqrt(HD)

    def one_block(running, block_inputs):
        key_grad, value_grad = running
        block_index, block_log = block_inputs
        row_start = block_index * token_total
        scores = (
            jnp.einsum("qhd,khd->hqk", queries, key_rows, preferred_element_type=jnp.float32)
            * score_scale
        )
        allowed = allowed_block(row_start, token_total, segment, is_valid)
        scores = jnp.where(allowed[None], scores, NEG_LARGE)
        prob_table = jnp.exp(scores - block_log[:, :, None])
        prob_low = prob_table.astype(jnp.bfloat16)
        value_grad = value_grad + jnp.einsum(
            "hqk,qhd->khd", prob_low, grad_att, preferred_element_type=jnp.float32
        )
        weight_grad = jnp.einsum(
            "qhd,khd->hqk", grad_att, values, preferred_element_type=jnp.float32
        )
        row_delta = jnp.transpose(
            jnp.sum(grad_att.astype(jnp.float32) * attended.astype(jnp.float32), axis=2)
        )
        score_grad = (prob_table * (weight_grad - row_delta[:, :, None]) * score_scale).astype(
            jnp.bfloat16
        )
        query_grad = jnp.einsum(
            "hqk,khd->qhd", score_grad, key_rows, preferred_element_type=jnp.float32
        )
        key_grad = key_grad + jnp.einsum(
            "hqk,qhd->khd", score_grad, queries, preferred_element_type=jnp.float32
        )
        return ((key_grad, value_grad), query_grad)

    zeros_grad = jnp.zeros((token_total, head_total, HD), jnp.float32)
    block_ids = jnp.arange(token_total // token_total, dtype=jnp.int32)
    (key_grad, value_grad), query_grad = lax.scan(
        one_block, (zeros_grad, zeros_grad), (block_ids, log_total)
    )
    return (query_grad.reshape(token_total, head_total, HD), key_grad, value_grad)


MESH = pl.DeviceIdType.MESH
VMEM_SPEC = pl.BlockSpec(memory_space=pltpu.VMEM)


def remote(src, dst, send_sem, recv_sem, target):
    return pltpu.make_async_remote_copy(
        src_ref=src, dst_ref=dst, send_sem=send_sem, recv_sem=recv_sem, device_id=target, device_id_type=MESH
    )


def greet(targets):
    barrier = pltpu.get_barrier_semaphore()
    for target in targets:
        pl.semaphore_signal(barrier, inc=1, device_id=target, device_id_type=MESH)
    pl.semaphore_wait(barrier, len(targets))


def row_exchange_kernel(kinds, n, *refs):
    count = len(kinds)
    ins, outs = refs[:count], refs[count : 2 * count]
    send, recv, own = refs[2 * count :]
    me = lax.axis_index("row")
    greet([{"row": lax.rem(me + d, n)} for d in range(1, n)])
    copies = []
    for i, kind in enumerate(kinds):
        for d in range(1, n):
            peer = lax.rem(me + d, n)
            piece = ins[i] if kind == "gather" else ins[i].at[peer]
            copy = remote(piece, outs[i].at[me], send.at[i, d - 1], recv.at[i, d - 1], {"row": peer})
            copy.start()
            copies.append(copy)
    for i, kind in enumerate(kinds):
        piece = ins[i] if kind == "gather" else ins[i].at[me]
        copy = pltpu.make_async_copy(piece, outs[i].at[me], own.at[i])
        copy.start()
        copies.append(copy)
    for copy in copies:
        copy.wait()


def row_exchange(kinds, arrays, collective_id):
    n = lax.axis_size("row")
    count = len(arrays)
    shapes = [(n,) + a.shape if k == "gather" else a.shape for k, a in zip(kinds, arrays)]
    return pl.pallas_call(
        functools.partial(row_exchange_kernel, kinds, n),
        out_shape=[jax.ShapeDtypeStruct(s, a.dtype) for s, a in zip(shapes, arrays)],
        in_specs=[VMEM_SPEC] * count,
        out_specs=[VMEM_SPEC] * count,
        scratch_shapes=[
            pltpu.SemaphoreType.DMA((count, n - 1)),
            pltpu.SemaphoreType.DMA((count, n - 1)),
            pltpu.SemaphoreType.DMA((count,)),
        ],
        compiler_params=pltpu.CompilerParams(collective_id=collective_id, has_side_effects=True),
    )(*arrays)


def group_places(n):
    r, c = lax.axis_index("row"), lax.axis_index("col")
    partner = c + 1 - 2 * lax.rem(c, 2)
    across = lax.rem(c + 2, 4)
    greet([{"row": lax.rem(r + d, n)} for d in range(1, n)] + [{"col": partner}, {"col": across}])
    return r, c, partner, across


def gather_kernel(n, x_ref, o_ref, own, zs, zr, ps, pr, ys, yr, fs, fr):
    r, c, partner, across = group_places(n)
    started = []
    mine = pltpu.make_async_copy(x_ref, o_ref.at[c, r], own)
    mine.start()
    hops = []
    for d in range(1, n):
        hop = remote(x_ref, o_ref.at[c, r], zs.at[d - 1], zr.at[d - 1], {"row": lax.rem(r + d, n)})
        hop.start()
        hops.append(hop)
    nears, fars = [], []
    for k in range(n):
        rk = lax.rem(r + n - k, n)
        if k:
            hops[k - 1].wait_recv()
        block = o_ref.at[c, rk] if k else x_ref
        far = remote(block, o_ref.at[c, rk], ys.at[k], yr.at[k], {"col": across})
        far.start()
        near = remote(block, o_ref.at[c, rk], ps.at[k], pr.at[k], {"col": partner})
        near.start()
        fars.append(far)
        nears.append(near)
    passed = []
    for k in range(n):
        rk = lax.rem(r + n - k, n)
        fars[k].wait_recv()
        on = remote(o_ref.at[across, rk], o_ref.at[across, rk], fs.at[k], fr.at[k], {"col": partner})
        on.start()
        passed.append(on)
    for copy in nears + passed:
        copy.wait_recv()
    for copy in hops + fars + nears + passed:
        copy.wait_send()
    mine.wait()


def gather_tokens(x, collective_id):
    n = lax.axis_size("row")
    return pl.pallas_call(
        functools.partial(gather_kernel, n),
        out_shape=jax.ShapeDtypeStruct((4, n) + x.shape, x.dtype),
        in_specs=[VMEM_SPEC],
        out_specs=VMEM_SPEC,
        scratch_shapes=[pltpu.SemaphoreType.DMA]
        + [pltpu.SemaphoreType.DMA((n - 1,))] * 2
        + [pltpu.SemaphoreType.DMA((n,))] * 6,
        compiler_params=pltpu.CompilerParams(collective_id=collective_id, has_side_effects=True),
    )(x)


def reduce_kernel(n, p_ref, o_ref, a_buf, b_out, b_in, c_out, c_in, a_s, a_r, b_s, b_r, c_s, c_r):
    r, c, partner, across = group_places(n)
    beyond = lax.rem(partner + 2, 4)
    firsts = []
    for slot, dest in ((1, beyond), (0, partner)):
        copy = remote(p_ref.at[dest], a_buf.at[slot], a_s.at[slot], a_r.at[slot], {"col": partner})
        copy.start()
        firsts.append(copy)
    order = list(range(1, n)) + [0]
    seconds = {}
    firsts[0].wait_recv()
    for d in order:
        k = lax.rem(r + d, n)
        b_out[d] = (p_ref[across, k].astype(jnp.float32) + a_buf[1, k].astype(jnp.float32)).astype(jnp.bfloat16)
        copy = remote(b_out.at[d], b_in.at[d], b_s.at[d], b_r.at[d], {"col": across})
        copy.start()
        seconds[d] = copy
    firsts[1].wait_recv()
    thirds = []
    total = None
    for d in order:
        k = lax.rem(r + d, n)
        seconds[d].wait_recv()
        total = p_ref[c, k].astype(jnp.float32) + a_buf[0, k].astype(jnp.float32) + b_in[d].astype(jnp.float32)
        if d:
            c_out[d - 1] = total.astype(jnp.bfloat16)
            copy = remote(c_out.at[d - 1], c_in.at[d - 1], c_s.at[d - 1], c_r.at[d - 1], {"row": k})
            copy.start()
            thirds.append(copy)
    o_ref[...] = total
    for d, copy in enumerate(thirds):
        copy.wait_recv()
        o_ref[...] += c_in[d].astype(jnp.float32)
    for copy in firsts + list(seconds.values()) + thirds:
        copy.wait_send()


def reduce_tokens(p, collective_id):
    n = lax.axis_size("row")
    block = p.shape[2:]
    low = jnp.bfloat16
    return pl.pallas_call(
        functools.partial(reduce_kernel, n),
        out_shape=jax.ShapeDtypeStruct(block, jnp.float32),
        in_specs=[VMEM_SPEC],
        out_specs=VMEM_SPEC,
        scratch_shapes=[
            pltpu.VMEM((2, n) + block, low),
            pltpu.VMEM((n,) + block, low),
            pltpu.VMEM((n,) + block, low),
            pltpu.VMEM((n - 1,) + block, low),
            pltpu.VMEM((n - 1,) + block, low),
            pltpu.SemaphoreType.DMA((2,)),
            pltpu.SemaphoreType.DMA((2,)),
            pltpu.SemaphoreType.DMA((n,)),
            pltpu.SemaphoreType.DMA((n,)),
            pltpu.SemaphoreType.DMA((n - 1,)),
            pltpu.SemaphoreType.DMA((n - 1,)),
        ],
        compiler_params=pltpu.CompilerParams(collective_id=collective_id, has_side_effects=True),
    )(p)


def sum_shards(array):
    if lax.axis_size("dp") == 2:
        other = lax.ppermute(array, "dp", [(0, 1), (1, 0)])
        return array.astype(jnp.float32) + other.astype(jnp.float32)
    return lax.psum(array, "dp").astype(jnp.float32)


def columns_first(matrix, n):
    return matrix.reshape(matrix.shape[0], n, -1).transpose(1, 0, 2)


def columns_last(pieces):
    return pieces.transpose(1, 0, 2).reshape(pieces.shape[1], -1)


def local(
    block_input, seq_lens, seq_offsets, ln_gain, ln_bias, w_qkv, w_attn_out, w_up, w_down, cotangent
):
    n = lax.axis_size("row")
    row = lax.axis_index("row")
    part = block_input.shape[1]
    held = block_input.shape[0] // n
    shard_tokens = block_input.shape[0] * lax.axis_size("col")
    segment, position, is_valid = token_layout(seq_lens[0], seq_offsets[0], shard_tokens)
    cosine_table, sine_table = rotary_tables(position)
    token_row = (jnp.arange(shard_tokens, dtype=jnp.int32) // held) % n
    is_mine = (token_row == row)[:, None]
    zero_low = jnp.zeros((), jnp.bfloat16)

    def weight_pieces(l):
        return [
            jnp.concatenate([w_qkv[l], w_attn_out[l]], axis=1),
            jnp.concatenate([columns_first(w_up[l], n), w_down[l].reshape(n, -1, part)], axis=2),
        ]

    def whole_weights(gathered, swapped):
        wide_part = gathered.shape[2] - part
        return (
            gathered[:, :, :wide_part].reshape(n * part, wide_part),
            columns_last(gathered[:, :, wide_part:]),
            swapped[:, :, : swapped.shape[2] - part].reshape(n * part, -1),
            columns_last(swapped[:, :, swapped.shape[2] - part :]),
        )

    norms = jnp.concatenate([ln_gain.reshape(-1, part), ln_bias.reshape(-1, part)], axis=0)
    ends = jnp.concatenate([block_input.reshape(n, held, part), cotangent.reshape(n, held, part)], axis=2)
    got = row_exchange(
        ("swap", "gather") + ("gather", "swap") * LAYERS,
        [ends, norms] + [piece for l in range(LAYERS) for piece in weight_pieces(l)],
        0,
    )
    residual = columns_last(got[0][:, :, :part])
    grad_state = columns_last(got[0][:, :, part:])
    norms = columns_last(got[1]).reshape(2, LAYERS, 2, -1)
    weights = [whole_weights(*got[2 + 2 * l : 4 + 2 * l]) for l in range(LAYERS)]
    gains, biases = norms[0], norms[1]

    saved = []
    grad_all = None
    for l in range(LAYERS):
        qkv_w, out_w, up_w, down_w = weights[l]
        mean = jnp.mean(residual, axis=1, keepdims=True)
        inv_std = lax.rsqrt(jnp.mean(residual * residual, axis=1, keepdims=True) - mean * mean + EPSILON)
        normed = (residual - mean) * inv_std
        normed_low = normed.astype(jnp.bfloat16)
        if l == 0:
            both = gather_tokens(jnp.stack([normed_low, grad_state.astype(jnp.bfloat16)]), 1)
            all_normed = both[:, :, 0].reshape(shard_tokens, -1)
            grad_all = both[:, :, 1].reshape(shard_tokens, -1)
        else:
            all_normed = gather_tokens(normed_low, 2).reshape(shard_tokens, -1)
        wide = all_normed.astype(jnp.float32)
        attn_in = (wide * gains[l, 0] + biases[l, 0]).astype(jnp.bfloat16)
        mlp_in = (wide * gains[l, 1] + biases[l, 1]).astype(jnp.bfloat16)
        proj = jnp.dot(attn_in, qkv_w, preferred_element_type=jnp.float32)
        pre = jnp.dot(mlp_in, up_w, preferred_element_type=jnp.float32)
        packed = rotary_pack(proj, cosine_table, sine_table)
        hidden = gelu_exact(pre).astype(jnp.bfloat16)
        queries, key_rows, values = split_heads(packed)
        attended, log_total = attend_forward(queries, key_rows, values, segment, is_valid)
        attended_flat = attended.reshape(shard_tokens, -1)
        branch = jnp.dot(
            jnp.where(is_mine, attended_flat, zero_low), out_w, preferred_element_type=jnp.float32
        ) + jnp.dot(hidden, down_w, preferred_element_type=jnp.float32)
        branch = branch.astype(jnp.bfloat16).reshape(-1, n, held, n * part)
        saved.append(
            (normed, inv_std, wide, attn_in, mlp_in, pre, queries, key_rows, values, attended_flat, log_total, hidden)
        )
        residual = residual + reduce_tokens(branch, 3)
    swap_list = [None] * LAYERS
    weight_list = [None] * LAYERS
    vector_list = [None] * LAYERS
    for l in reversed(range(LAYERS)):
        (normed, inv_std, wide, attn_in, mlp_in, pre, queries, key_rows, values, attended_flat, log_total, hidden) = saved[l]
        qkv_w, out_w, up_w, down_w = weights[l]
        heads = queries.shape[1]
        if l < LAYERS - 1:
            grad_all = gather_tokens(grad_state.astype(jnp.bfloat16), 2).reshape(shard_tokens, -1)
        my_grad = lax.dynamic_slice_in_dim(grad_all, row * part, part, 1)
        grad_out_w = jnp.dot(attended_flat.T, my_grad, preferred_element_type=jnp.float32)
        grad_down_w = jnp.dot(hidden.T, grad_all, preferred_element_type=jnp.float32)
        grad_att = jnp.dot(grad_all, out_w.T, preferred_element_type=jnp.float32).astype(jnp.bfloat16)
        grad_hidden = jnp.dot(grad_all, down_w.T, preferred_element_type=jnp.float32)
        grad_pre = (grad_hidden * gelu_slope(pre)).astype(jnp.bfloat16)
        query_grad, key_grad, value_grad = attend_backward(
            queries,
            key_rows,
            values,
            attended_flat.reshape(shard_tokens, heads, HD),
            grad_att.reshape(shard_tokens, heads, HD),
            log_total,
            segment,
            is_valid,
        )
        query_grad = rotate_pairs(query_grad, cosine_table, sine_table, -1.0)
        key_grad = rotate_pairs(key_grad, cosine_table, sine_table, -1.0)
        grad_proj = (
            jnp.stack([query_grad, key_grad, value_grad], axis=2).reshape(shard_tokens, -1).astype(jnp.bfloat16)
        )
        my_attn_in = lax.dynamic_slice_in_dim(attn_in, row * part, part, 1)
        grad_qkv_w = jnp.dot(my_attn_in.T, grad_proj, preferred_element_type=jnp.float32)
        grad_up_w = jnp.dot(mlp_in.T, grad_pre, preferred_element_type=jnp.float32)
        grad_attn_in = jnp.dot(
            jnp.where(is_mine, grad_proj, zero_low), qkv_w.T, preferred_element_type=jnp.float32
        )
        grad_mlp_in = jnp.dot(grad_pre, up_w.T, preferred_element_type=jnp.float32)
        weight_list[l] = (
            sum_shards(grad_qkv_w.astype(jnp.bfloat16)),
            sum_shards(grad_out_w.astype(jnp.bfloat16)),
        )
        pieces = jnp.concatenate(
            [
                grad_up_w.astype(jnp.bfloat16).reshape(n, part, -1),
                columns_first(grad_down_w.astype(jnp.bfloat16), n),
            ],
            axis=2,
        )
        swap_list[l] = sum_shards(pieces).astype(jnp.bfloat16)
        vector_list[l] = jnp.stack(
            [
                jnp.sum(grad_attn_in * wide, axis=0),
                jnp.sum(grad_mlp_in * wide, axis=0),
                jnp.sum(grad_attn_in, axis=0),
                jnp.sum(grad_mlp_in, axis=0),
            ]
        )
        mixed = (grad_attn_in * gains[l, 0] + grad_mlp_in * gains[l, 1]).astype(jnp.bfloat16)
        grad_normed = reduce_tokens(mixed.reshape(-1, n, held, n * part), 3)
        plain_mean = jnp.mean(grad_normed, axis=1, keepdims=True)
        cross_mean = jnp.mean(grad_normed * normed, axis=1, keepdims=True)
        grad_state = grad_state + inv_std * (grad_normed - plain_mean - normed * cross_mean)
    ends = jnp.concatenate([columns_first(residual, n), columns_first(grad_state, n)], axis=2)
    vectors = sum_shards(jnp.concatenate(vector_list, axis=0))
    got = row_exchange(("swap",) * (2 + LAYERS), [columns_first(vectors, n), ends] + swap_list, 4)
    vectors = jnp.sum(got[0], axis=0)
    got = got[1:]
    col_count = lax.axis_size("col")
    vectors = vectors + sum(
        lax.ppermute(vectors, "col", [(i, (i + d) % col_count) for i in range(col_count)])
        for d in range(1, col_count)
    )
    vectors = vectors.reshape(LAYERS, 4, part)
    output = got[0][:, :, :part].reshape(-1, part)
    final_grad = got[0][:, :, part:].reshape(-1, part)
    totals = [
        jnp.stack([w[0] for w in weight_list]),
        jnp.stack([w[1] for w in weight_list]),
        jnp.stack([columns_last(g[:, :, : g.shape[2] - part]) for g in got[1:]]).astype(jnp.float32),
        jnp.stack([g[:, :, g.shape[2] - part :].reshape(-1, part) for g in got[1:]]).astype(jnp.float32),
    ]
    return (output, final_grad, vectors[:, :2], vectors[:, 2:], *totals)


def solution(mesh):
    return jax.shard_map(
        local,
        mesh=mesh,
        in_specs=(
            P(("dp", "col"), "row"),
            P("dp", None),
            P("dp", None),
            P(None, None, "row"),
            P(None, None, "row"),
            P(None, "row", "col"),
            P(None, "col", "row"),
            P(None, "row", "col"),
            P(None, "col", "row"),
            P(("dp", "col"), "row"),
        ),
        out_specs=(
            P(("dp", "col"), "row"),
            P(("dp", "col"), "row"),
            P(None, None, "row"),
            P(None, None, "row"),
            P(None, "row", "col"),
            P(None, "col", "row"),
            P(None, "row", "col"),
            P(None, "col", "row"),
        ),
        check_vma=False,
    )
```
